512 devices in a mesh: tm: 16 (over z_lo, x, core), height: 32 (over y, z_hi).
Axes of the slice: x: 4, y: 8, z: 8 (z_hi: 4, z_lo: 2; z = z_hi * 2 + z_lo), core: 2. Of those that a mesh axis runs over, the one named last changes fastest.
Arguments:
- video_q: bfloat16 [16, 32, 768, 256], P('tm', 'height'), may hold values from -4.5 to 4.5
- video_k: bfloat16 [16, 32, 768, 256], P('tm', 'height'), may hold values from -4.5 to 4.5
- video_v: bfloat16 [16, 32, 768, 256], P('tm', 'height'), may hold values from -6 to 6
- text_k: bfloat16 [256, 256], P('height'), may hold values from -4.5 to 4.5
- text_v: bfloat16 [256, 256], P('height'), may hold values from -6 to 6
- text_valid: int32 [256], replicated, may hold values from 0 to 1, as said below
- extent: int32 [2, 3], replicated, may hold values from 0 to 1
Outputs:
- video_out: bfloat16 [16, 32, 768, 256], P('tm', 'height')
The draws below stay inside these ranges and needn't reach their ends.
Inputs may be any that keep to these rules, and one draw needn't show every extreme that they name: `text_valid`: the valid text tokens come first; at least 64 are valid and at least one is not.
All inputs are finite; a program needn't handle non-finite values.
Results may differ from the reference program's by a relative error of at most 0.0042.
Values may be sent and summed in bfloat16 or wider, within the bound.
No kernel may reach another device: no remote copies, remote signals or barrier semaphores. Data moves between devices by JAX's collectives and lax.ppermute only.
A program may use at most 64 MiB of HBM per device.

```python
import math
import jax
import jax.numpy as jnp
from jax import lax

HEADS = 2
TILE = 384
WT = 2
TEXT = 256
FEAT = 256
TIME_TILES = 16
HEIGHT_TILES = 32
TIME_ROWS = 16
HEIGHT_ROWS = 32


def base_field(key, salt, shape, spread):
    subkey = jax.random.fold_in(key, salt)
    values = jax.random.normal(subkey, shape, jnp.float32) * spread
    return jnp.clip(values, -4.5, 4.5)


def draw_video_q(key, part):
    shape = (TIME_ROWS, HEIGHT_ROWS, WT * TILE, FEAT)
    values = base_field(key, 11, shape, 1.0)
    return values.astype(jnp.bfloat16)


def draw_video_k(key, part):
    shape = (TIME_ROWS, HEIGHT_ROWS, WT * TILE, FEAT)
    values = base_field(key, 12, shape, 1.5)
    return values.astype(jnp.bfloat16)


def draw_text_valid(key, part):
    length = jax.random.randint(jax.random.fold_in(key, 21), (), TEXT // 4, TEXT)
    return (jnp.arange(TEXT, dtype=jnp.int32) < length).astype(jnp.int32)


def draw_extent(key, part):
    values = jax.random.randint(jax.random.fold_in(key, 31), (HEADS, 3), 0, 2)
    chosen = jax.random.randint(jax.random.fold_in(key, 32), (3,), 0, HEADS)
    offset = jax.random.randint(jax.random.fold_in(key, 33), (3,), 1, HEADS)
    other = (chosen + offset) % HEADS
    head_ids = jnp.arange(HEADS, dtype=jnp.int32)[:, None]
    values = jnp.where(head_ids == chosen[None, :], 1, jnp.where(head_ids == other[None, :], 0, values))
    return values.astype(jnp.int32)


def steps_of(own_key, shape, split, smallest, top_value):
    level, own = 1.0, jax.random.fold_in(own_key, 6)
    for dim, shards_of in split:
        heights = jnp.exp(jax.random.uniform(jax.random.fold_in(own, dim), (shards_of,), jnp.float32, smallest / len(split), top_value / len(split)))
        level = level * jnp.repeat(heights, shape[dim] // shards_of).reshape([-1 if axis == dim else 1 for axis in range(len(shape))])
    return level


def scatter_about(key, shape, scale, limit, shards=(), held_as=jnp.bfloat16):
    loudness = steps_of(key, shape, shards, -0.22, 0.18) if shards else 1.0
    array = jax.random.normal(key, shape, jnp.float32) * scale * loudness
    return jnp.minimum(jnp.maximum(array, -limit), limit).astype(held_as)


def setup_inputs(seed: int = 0) -> dict:
    key_of = jax.random.split(jax.random.key(seed), 8)
    return {
        "video_q": draw_video_q(jax.random.fold_in(key_of[7], 71), 0),
        "video_k": draw_video_k(jax.random.fold_in(key_of[7], 71), 0),
        "video_v": scatter_about(key_of[2], (TIME_ROWS, HEIGHT_ROWS, WT * TILE, FEAT), 1.0, 6.0, ((0, 16), (1, 32))),
        "text_k": scatter_about(key_of[3], (TEXT, FEAT), 1.5, 4.5, ((0, 32),)),
        "text_v": scatter_about(key_of[4], (TEXT, FEAT), 1.0, 6.0, ((0, 32),)),
        "text_valid": draw_text_valid(jax.random.fold_in(key_of[7], 71), 0),
        "extent": draw_extent(jax.random.fold_in(key_of[7], 71), 0),
    }


def tile_output(query_rows, slab_keys, slab_values, inside, text_k, text_v, text_ok, extent):
    row_count = query_rows.shape[0]
    feat_count = query_rows.shape[1]
    head_count = extent.shape[0]
    head_width = feat_count // head_count
    tile_count = row_count // TILE
    score_scale = 1.0 / math.sqrt(head_width)
    key_ids = jnp.arange(9 * row_count, dtype=jnp.int32)
    slab_index = key_ids // row_count
    time_gap = slab_index // 3 - 1
    height_gap = slab_index % 3 - 1
    key_tile = key_ids % row_count // TILE
    inside_keys = inside[slab_index]
    queries = query_rows.reshape(tile_count, TILE, feat_count)

    def one_block(operands):
        query_block, query_tile = operands
        width_gap = jnp.abs(key_tile - query_tile)
        head_outputs = []
        for head_index in range(head_count):
            low = head_index * head_width
            high = low + head_width
            allowed = inside_keys & (jnp.abs(time_gap) <= extent[head_index, 0]) & (jnp.abs(height_gap) <= extent[head_index, 1])
            allowed = allowed & (width_gap <= extent[head_index, 2])
            query_head = query_block[:, low:high]
            video_scores = jnp.dot(query_head, slab_keys[:, low:high].T, preferred_element_type=jnp.float32) * score_scale
            text_scores = jnp.dot(query_head, text_k[:, low:high].T, preferred_element_type=jnp.float32) * score_scale
            video_scores = jnp.where(allowed[None, :], video_scores, -jnp.inf)
            text_scores = jnp.where(text_ok[None, :], text_scores, -jnp.inf)
            row_top = jnp.maximum(lax.optimization_barrier(jnp.max(video_scores, axis=1)), lax.optimization_barrier(jnp.max(text_scores, axis=1)))
            video_expo = jnp.exp(video_scores - row_top[:, None])
            text_expo = jnp.exp(text_scores - row_top[:, None])
            row_total = lax.optimization_barrier(jnp.sum(video_expo, axis=1)) + lax.optimization_barrier(jnp.sum(text_expo, axis=1))
            weighted = jnp.dot(video_expo.astype(jnp.bfloat16), slab_values[:, low:high], preferred_element_type=jnp.float32)
            weighted = weighted + jnp.dot(text_expo.astype(jnp.bfloat16), text_v[:, low:high], preferred_element_type=jnp.float32)
            head_outputs.append(weighted / row_total[:, None])
        return jnp.concatenate(head_outputs, axis=1).astype(jnp.bfloat16)
    blocks = lax.map(one_block, (queries, jnp.arange(tile_count, dtype=jnp.int32)))
    return blocks.reshape(row_count, feat_count)

def reference(video_q, video_k, video_v, text_k, text_v, text_valid, extent):
    text_ok = text_valid > 0

    def one_tile(flat_index):
        time_row = flat_index // HEIGHT_ROWS
        height_row = flat_index % HEIGHT_ROWS
        local_time = time_row % TIME_TILES
        local_height = height_row % HEIGHT_TILES
        key_parts = []
        value_parts = []
        inside_parts = []
        for time_shift in (-1, 0, 1):
            for height_shift in (-1, 0, 1):
                source_time = jnp.clip(time_row + time_shift, 0, TIME_ROWS - 1).astype(jnp.int32)
                source_height = jnp.clip(height_row + height_shift, 0, HEIGHT_ROWS - 1).astype(jnp.int32)
                key_row = lax.dynamic_index_in_dim(video_k, source_time, 0, False)
                key_parts.append(lax.dynamic_index_in_dim(key_row, source_height, 0, False))
                value_row = lax.dynamic_index_in_dim(video_v, source_time, 0, False)
                value_parts.append(lax.dynamic_index_in_dim(value_row, source_height, 0, False))
                inside_parts.append((local_time + time_shift >= 0) & (local_time + time_shift < TIME_TILES) & (local_height + height_shift >= 0) & (local_height + height_shift < HEIGHT_TILES))
        slab_keys = jnp.concatenate(key_parts, axis=0)
        slab_values = jnp.concatenate(value_parts, axis=0)
        inside = jnp.stack(inside_parts)
        query_row = lax.dynamic_index_in_dim(video_q, time_row.astype(jnp.int32), 0, False)
        query_rows = lax.dynamic_index_in_dim(query_row, height_row.astype(jnp.int32), 0, False)
        return tile_output(query_rows, slab_keys, slab_values, inside, text_k, text_v, text_ok, extent)
    flat_ids = jnp.arange(TIME_ROWS * HEIGHT_ROWS, dtype=jnp.int32)
    tiles = lax.map(one_tile, flat_ids)
    return tiles.reshape(video_q.shape)
```

```python
import functools
import math

import jax
import jax.numpy as jnp
from jax import lax
from jax.experimental import pallas as pl
from jax.experimental.pallas import tpu as pltpu
from jax.sharding import PartitionSpec as P


TILE = 384
HW = 128
NEG = -1e30
SUB = 128


def rings(axis):
    size = lax.axis_size(axis)
    up = [(i, i + 1) for i in range(size - 1)]
    return up, [(j, i) for i, j in up]


def attention_kernel(spec, *refs):
    jobs, has_own, ends, slabs, n_slab_refs, paired, scale = spec
    refs = list(refs)
    ext_ref, q_ref = refs[:2]
    refs = refs[2:]
    if has_own:
        k_ref, v_ref, text_ref, valid_ref = refs[:4]
        refs = refs[4:]
    else:
        mi_ref, li_ref, ai_ref = refs[:3]
        refs = refs[3:]
    slab_refs = refs[:n_slab_refs]
    refs = refs[n_slab_refs:]
    if ends == "merge":
        other_ref = refs.pop(0)
    if ends == "state":
        mo_ref, lo_ref, ao_ref = refs[:3]
        refs = refs[3:]
    elif ends == "split":
        mo_ref, lo_ref, ao_ref, oo_ref = refs[:4]
        refs = refs[4:]
    else:
        out_ref = refs.pop(0)
    m_ref, l_ref, a_ref = refs
    row_count = q_ref.shape[0]
    tiles = row_count // TILE
    time_at, height_at = lax.axis_index("tm"), lax.axis_index("height")
    height_head = 1 - ext_ref[0, 1]

    def one_tile(step, carry):
        job, w = step // tiles, step % tiles
        head = jnp.where(job == 0, height_head, 1 - height_head)
        low = pl.multiple_of(head * HW, HW)
        wide = ext_ref[head, 2] > 0
        base = pl.multiple_of(w * TILE, TILE)
        rows = pl.ds(base, TILE)

        def attend(k, v, first=False, valid=None):
            for s0 in range(0, TILE, SUB):
                sub = pl.ds(s0, SUB)
                q = q_ref[pl.ds(base + s0, SUB), pl.ds(low, HW)]
                s = lax.dot_general(
                    q, k, (((1,), (1,)), ((), ())), preferred_element_type=jnp.float32
                )
                if valid is not None:
                    s = jnp.where(valid, s, NEG)
                top = jnp.max(s, axis=1, keepdims=True)
                if first:
                    m_new = jnp.broadcast_to(top, (SUB, HW))
                else:
                    m_old = m_ref[sub, :]
                    m_new = jnp.maximum(m_old, top)
                    alpha = jnp.exp2((m_old - m_new) * scale)
                m_ref[sub, :] = m_new
                parts = []
                total = None
                for c in range(0, s.shape[1], HW):
                    p = jnp.exp2((s[:, c : c + HW] - m_new) * scale)
                    total = p if total is None else total + p
                    parts.append(p.astype(jnp.bfloat16))
                p = jnp.concatenate(parts, axis=1)
                pv = jnp.dot(p, v, preferred_element_type=jnp.float32)
                if first:
                    l_ref[sub, :] = total
                    a_ref[sub, :] = pv
                else:
                    l_ref[sub, :] = l_ref[sub, :] * alpha + total
                    a_ref[sub, :] = a_ref[sub, :] * alpha + pv

        def slab(kr, vr, row0, kc, vc, first=False):
            @pl.when(wide)
            def _():
                at = pl.ds(pl.multiple_of(row0, TILE), row_count)
                attend(kr[at, pl.ds(kc, HW)], vr[at, pl.ds(vc, HW)], first)

            @pl.when(jnp.logical_not(wide))
            def _():
                at = pl.ds(pl.multiple_of(row0 + base, TILE), TILE)
                attend(kr[at, pl.ds(kc, HW)], vr[at, pl.ds(vc, HW)], first)

        if has_own:
            slab(k_ref, v_ref, 0, low, low, True)
            attend(
                text_ref[:, pl.ds(low, HW)],
                text_ref[:, pl.ds(pl.multiple_of(low + 2 * HW, HW), HW)],
                valid=valid_ref[...] > 0,
            )
        else:
            m_ref[...] = mi_ref[rows, :]
            l_ref[...] = li_ref[rows, :]
            a_ref[...] = ai_ref[rows, :]

        for ref_id, count, dt, dh in slabs:
            ref = slab_refs[ref_id]
            kc = low if paired else 0
            vc = pl.multiple_of(low + 2 * HW, HW) if paired else HW

            def one_slab(i, carry, ref=ref, dt=dt, dh=dh, kc=kc, vc=vc):
                time, height = time_at + dt, height_at + dh + i
                held = (time >= 0) & (time < lax.axis_size("tm"))
                held = held & (height >= 0) & (height < lax.axis_size("height"))
                if dt != 0:
                    held = held & (ext_ref[head, 0] > 0)
                held = held & (jnp.abs(dh + i) <= ext_ref[head, 1])

                @pl.when(held)
                def _():
                    slab(ref, ref, i * row_count, kc, vc)

                return carry

            if count == 1:
                one_slab(0, 0)
            else:
                lax.fori_loop(0, count, one_slab, 0)

        def keep():
            mo_ref[rows, :] = m_ref[...]
            lo_ref[rows, :] = l_ref[...]
            ao_ref[rows, :] = a_ref[...]

        def finish(ref, cols):
            total = jnp.sum(l_ref[...], axis=1, keepdims=True)
            ref[rows, cols] = (a_ref[...] / total).astype(jnp.bfloat16)

        if ends == "state":
            keep()
        elif ends == "split":
            pl.when(job == 0)(keep)
            pl.when(job != 0)(lambda: finish(oo_ref, pl.ds(0, HW)))
        else:
            finish(out_ref, pl.ds(low, HW))
            if ends == "merge":
                cols = pl.ds(pl.multiple_of((1 - head) * HW, HW), HW)
                out_ref[rows, cols] = other_ref[rows, :]
        return carry

    lax.fori_loop(0, jobs * tiles, one_tile, 0)


SMEM = pl.BlockSpec(memory_space=pltpu.SMEM)
VMEM = pl.BlockSpec(memory_space=pltpu.VMEM)


def attention(jobs, ends, slabs, ext, q, arrays, own=None, state=None, other=None, paired=False):
    rows, feat = q.shape
    scale = math.log2(math.e) / math.sqrt(HW)
    spec = (jobs, own is not None, ends, slabs, len(arrays), paired, scale)
    args = [ext, q] + list(own if own is not None else state) + list(arrays)
    if other is not None:
        args.append(other)
    part = jax.ShapeDtypeStruct((rows, HW), jnp.float32)
    if ends == "state":
        outs = (part,) * 3
    elif ends == "split":
        outs = (part,) * 3 + (jax.ShapeDtypeStruct((rows, HW), jnp.bfloat16),)
    else:
        outs = jax.ShapeDtypeStruct((rows, feat), jnp.bfloat16)
    scores = rows * rows * (sum(s[1] for s in slabs) + 1)
    return pl.pallas_call(
        functools.partial(attention_kernel, spec),
        out_shape=outs,
        in_specs=[SMEM] + [VMEM] * (len(args) - 1),
        out_specs=(VMEM,) * len(outs) if isinstance(outs, tuple) else VMEM,
        scratch_shapes=[pltpu.VMEM((TILE, HW), jnp.float32)] * 3,
        compiler_params=pltpu.CompilerParams(vmem_limit_bytes=40 * 1024 * 1024),
        cost_estimate=pl.CostEstimate(
            flops=4 * HW * scores, bytes_accessed=4 * rows * feat * 4, transcendentals=scores
        ),
    )(*args)


def pick_kernel(ext_ref, k_ref, v_ref, out_ref):
    out_ref[:, :HW] = k_ref[...]
    out_ref[:, HW:] = v_ref[...]


def of_head(ext, k, v, axis):
    rows = k.shape[0]
    part = pl.BlockSpec((rows, HW), lambda i, ext_ref: (0, 1 - ext_ref[0, axis]))
    return pl.pallas_call(
        pick_kernel,
        grid_spec=pltpu.PrefetchScalarGridSpec(
            num_scalar_prefetch=1,
            grid=(1,),
            in_specs=[part, part],
            out_specs=pl.BlockSpec((rows, 2 * HW), lambda i, ext_ref: (0, 0)),
        ),
        out_shape=jax.ShapeDtypeStruct((rows, 2 * HW), k.dtype),
        cost_estimate=pl.CostEstimate(flops=0, bytes_accessed=8 * rows * HW, transcendentals=0),
    )(ext, k, v)


def shards(video_q, video_k, video_v, text_k, text_v, text_valid, extent):
    rows, feat = video_q.shape[2:]
    q, k, v = (a.reshape(rows, feat) for a in (video_q, video_k, video_v))
    hn = lax.axis_size("height")
    t_rings, h_rings = rings("tm"), rings("height")
    valid = text_valid.reshape(1, -1)

    table = 0
    for c in range(16):
        t0, h0, t1, h1 = (c >> i & 1 for i in range(4))
        crowded = (t0 and t1) or (h0 and h1)
        table |= (2 if crowded else int((t0 and h0) or (t1 and h1))) << (2 * c)
    table -= (table >> 31) << 32
    shift = jnp.sum(extent * jnp.array([[2, 4, 0], [8, 16, 0]], jnp.int32))
    branch = lax.shift_right_arithmetic(jnp.int32(table), shift) & 3

    def text_tokens(text_k, text_v):
        mine = jnp.concatenate([text_k, text_v], axis=1)
        copies = jnp.broadcast_to(mine[None], (hn,) + mine.shape)
        got = lax.all_to_all(copies, "height", 0, 0)
        return got.reshape(-1, mine.shape[1])

    def exchange(x, axis, pairs):
        up, down = pairs
        before = lax.ppermute(x, axis, up)
        after = lax.ppermute(x, axis, down)
        return before, after

    def sparse(diagonal):
        def run(q, k, v, text_k, text_v, valid, ext):
            kv_h = of_head(ext, k, v, 1)
            h0, h1 = exchange(kv_h, "height", h_rings)
            kv_t = of_head(ext, k, v, 0)
            t0, t1 = exchange(kv_t, "tm", t_rings)
            text = text_tokens(text_k, text_v)
            m, l, a, other = attention(
                2, "split", ((0, 1, -1, 0), (1, 1, 1, 0)),
                ext, q, (t0, t1), own=(k, v, text, valid),
            )
            hs = ((0, 1, 0, -1), (1, 1, 0, 1))
            if not diagonal:
                return attention(1, "merge", hs, ext, q, (h0, h1), state=(m, l, a), other=other)
            d00, d10 = exchange(h0, "tm", t_rings)
            d01, d11 = exchange(h1, "tm", t_rings)
            m, l, a = attention(1, "state", hs, ext, q, (h0, h1), state=(m, l, a))
            ds = ((0, 1, -1, -1), (1, 1, 1, -1), (2, 1, -1, 1), (3, 1, 1, 1))
            return attention(
                1, "merge", ds, ext, q, (d00, d10, d01, d11),
                state=(m, l, a), other=other,
            )

        return run

    def dense(q, k, v, text_k, text_v, valid, ext):
        kv = jnp.concatenate([k, v], axis=1)
        h0, h1 = exchange(kv, "height", h_rings)
        text = text_tokens(text_k, text_v)
        three = jnp.concatenate([h0, kv, h1], axis=0)
        t0, t1 = exchange(three, "tm", t_rings)
        slabs = ((0, 1, 0, -1), (1, 1, 0, 1), (2, 3, -1, -1), (3, 3, 1, -1))
        return attention(
            2, "all", slabs, ext, q, (h0, h1, t0, t1),
            own=(k, v, text, valid), paired=True,
        )

    out = lax.switch(
        branch, [sparse(False), sparse(True), dense], q, k, v, text_k, text_v, valid, extent
    )
    return out.reshape(video_q.shape)


def solution(mesh):
    video = P("tm", "height", None, None)
    return jax.shard_map(
        shards,
        mesh=mesh,
        in_specs=(video, video, video, P("height", None), P("height", None), P(), P()),
        out_specs=video,
        check_vma=False,
    )
```

```python
import functools
import math

import jax
import jax.numpy as jnp
from jax import lax
from jax.experimental import pallas as pl
from jax.experimental.pallas import tpu as pltpu
from jax.sharding import PartitionSpec as P


TILE = 384
HW = 128
NEG = -1e30
MARK = 1e30
SLOW = 128


def rings(axis):
    size = lax.axis_size(axis)
    up = [(i, i + 1) for i in range(size - 1)]
    return up, [(j, i) for i, j in up]


def attention_kernel(spec, *refs):
    jobs, has_own, ends, slabs, n_slab_refs, paired, scale = spec
    refs = list(refs)
    ext_ref, q_ref = refs[:2]
    refs = refs[2:]
    if has_own:
        k_ref, v_ref, text_ref, valid_ref = refs[:4]
        refs = refs[4:]
    else:
        mi_ref, li_ref, ai_ref = refs[:3]
        refs = refs[3:]
    slab_refs = refs[:n_slab_refs]
    refs = refs[n_slab_refs:]
    if ends == "merge":
        other_ref = refs.pop(0)
    if ends == "state":
        mo_ref, lo_ref, ao_ref = refs[:3]
        refs = refs[3:]
    elif ends == "split":
        mo_ref, lo_ref, ao_ref, oo_ref = refs[:4]
        refs = refs[4:]
    else:
        out_ref = refs.pop(0)
    m_ref, l_ref, a_ref = refs
    row_count = q_ref.shape[0]
    tiles = row_count // TILE
    time_at, height_at = lax.axis_index("tm"), lax.axis_index("height")
    height_head = 1 - ext_ref[0, 1]
    compact = ends == "all"

    def reaches(head, along_time, along_height):
        needed = jnp.bool_(True)
        if along_time:
            needed = needed & (ext_ref[head, 0] > 0)
        if along_height:
            needed = needed & (ext_ref[head, 1] > 0)
        return needed

    def one_head(job, carry):
        head = jnp.where(job == 0, height_head, 1 - height_head)
        low = pl.multiple_of(head * HW, HW)
        high = pl.multiple_of(low + 2 * HW, HW)
        wide = ext_ref[head, 2] > 0
        q_cols = pl.ds(low, HW)

        def fast(row, count, k, v, held=None, valid=None, base=(l_ref, a_ref)):
            at = pl.ds(row, count)
            s = lax.dot_general(
                q_ref[at, q_cols], k, (((1,), (1,)), ((), ())),
                preferred_element_type=jnp.float32,
            )
            parts = []
            total = None
            for c in range(0, s.shape[1], HW):
                p = jnp.exp2(s[:, c : c + HW] * scale)
                if valid is not None:
                    p = jnp.where(valid[:, c : c + HW], p, 0.0)
                total = p if total is None else total + p
                parts.append(p.astype(jnp.bfloat16))
            if held is not None:
                total = total * held
            pv = jnp.dot(
                jnp.concatenate(parts, axis=1), v, preferred_element_type=jnp.float32
            )
            l_ref[at, :] = total if base is None else base[0][at, :] + total
            a_ref[at, :] = pv if base is None else base[1][at, :] + pv

        def slow(row, k, v, valid=None):
            def one_sub(i, carry):
                sub = pl.ds(pl.multiple_of(row + i * SLOW, SLOW), SLOW)
                s = lax.dot_general(
                    q_ref[sub, q_cols], k, (((1,), (1,)), ((), ())),
                    preferred_element_type=jnp.float32,
                )
                if valid is not None:
                    s = jnp.where(valid, s, NEG)
                m_old = m_ref[sub, :]
                m_new = jnp.maximum(m_old, jnp.max(s, axis=1, keepdims=True))
                alpha = jnp.exp2((m_old - m_new) * scale)
                p = jnp.exp2((s - m_new[:, :1]) * scale)
                total = sum(p[:, c : c + HW] for c in range(0, s.shape[1], HW))
                m_ref[sub, :] = m_new
                l_ref[sub, :] = l_ref[sub, :] * alpha + total
                a_ref[sub, :] = a_ref[sub, :] * alpha + jnp.dot(
                    p.astype(jnp.bfloat16), v, preferred_element_type=jnp.float32
                )
                return carry

            lax.fori_loop(0, TILE // SLOW, one_sub, 0)

        if has_own:
            reach = jnp.abs(q_ref[:, q_cols].astype(jnp.float32))
            safe = jnp.max(jnp.sum(reach, axis=1, keepdims=True)) * (4.5 * scale) < 90.0
        else:
            safe = mi_ref[0, 0] > MARK / 2
        unsafe = jnp.logical_not(safe)

        def group(needed, members, base=(l_ref, a_ref)):
            def whole(row, count, shift):
                start = base
                for kr, vr, row0, kc, vc, held in members:
                    at = pl.ds(row0 + shift, count)
                    held = None if held is None else held.astype(jnp.float32)
                    k, v = kr[at, pl.ds(kc, HW)], vr[at, pl.ds(vc, HW)]
                    fast(row, count, k, v, held, base=start)
                    start = (l_ref, a_ref)

            def one_pair(i, carry):
                w, w2 = i // tiles, i % tiles
                row = pl.multiple_of(w * TILE, TILE)
                for kr, vr, row0, kc, vc, held in members:
                    seen = wide | (w2 == w)
                    seen = seen if held is None else seen & (held > 0)
                    at = pl.ds(pl.multiple_of(row0 + w2 * TILE, TILE), TILE)

                    @pl.when(seen & unsafe)
                    def _(kr=kr, vr=vr, at=at, kc=kc, vc=vc):
                        slow(row, kr[at, pl.ds(kc, HW)], vr[at, pl.ds(vc, HW)])

                    if compact:

                        @pl.when(seen & safe)
                        def _(kr=kr, vr=vr, at=at, kc=kc, vc=vc):
                            fast(row, TILE, kr[at, pl.ds(kc, HW)], vr[at, pl.ds(vc, HW)])

                return carry

            @pl.when(needed if compact else needed & unsafe)
            def _():
                lax.fori_loop(0, tiles * tiles, one_pair, 0)

            if not compact:
                pl.when(needed & safe & wide)(lambda: whole(0, row_count, 0))

                @pl.when(needed & safe & jnp.logical_not(wide))
                def _():
                    for w in range(tiles):
                        whole(w * TILE, TILE, w * TILE)

        if has_own:

            @pl.when(jnp.bool_(True) if compact else unsafe)
            def _():
                l_ref[...] = jnp.zeros_like(l_ref)
                a_ref[...] = jnp.zeros_like(a_ref)
                m_ref[...] = jnp.full_like(m_ref, NEG)

            group(jnp.bool_(True), [(k_ref, v_ref, 0, low, low, None)], base=None)

            @pl.when(safe)
            def _():
                fast(0, row_count, text_ref[:, q_cols], text_ref[:, pl.ds(high, HW)], None, valid_ref[...] > 0)

            @pl.when(unsafe)
            def _():
                def one_tile(w, carry):
                    slow(w * TILE, text_ref[:, q_cols], text_ref[:, pl.ds(high, HW)], valid_ref[...] > 0)
                    return carry

                lax.fori_loop(0, tiles, one_tile, 0)
        else:
            ((along_time, along_height, _),) = slabs
            needed = reaches(head, along_time, along_height)

            @pl.when(unsafe | jnp.logical_not(needed))
            def _():
                m_ref[...] = mi_ref[...]
                l_ref[...] = li_ref[...]
                a_ref[...] = ai_ref[...]

        for along_time, along_height, members in slabs:
            needed = reaches(head, along_time, along_height)
            found = []
            for ref_id, row0, dt, dh in members:
                time, height = time_at + dt, height_at + dh
                held = (time >= 0) & (time < lax.axis_size("tm"))
                held = held & (height >= 0) & (height < lax.axis_size("height"))
                ref = slab_refs[ref_id]
                cols = (low, high) if paired else (0, HW)
                found.append((ref, ref, row0) + cols + (held.astype(jnp.int32),))
            group(needed, found, (l_ref, a_ref) if has_own else (li_ref, ai_ref))

        def keep():
            @pl.when(unsafe)
            def _():
                mo_ref[...] = m_ref[...]

            @pl.when(safe)
            def _():
                mo_ref[0:8, :] = jnp.full((8, HW), MARK, jnp.float32)

            lo_ref[...] = l_ref[...]
            ao_ref[...] = a_ref[...]

        def finish(ref, cols):
            total = jnp.sum(l_ref[...], axis=1, keepdims=True)
            ref[:, cols] = (a_ref[...] / total).astype(jnp.bfloat16)

        if ends == "state":
            keep()
        elif ends == "split":
            pl.when(job == 0)(keep)
            pl.when(job != 0)(lambda: finish(oo_ref, pl.ds(0, HW)))
        else:
            finish(out_ref, q_cols)
            if ends == "merge":
                cols = pl.ds(pl.multiple_of((1 - head) * HW, HW), HW)
                out_ref[:, cols] = other_ref[...]
        return carry

    lax.fori_loop(0, jobs, one_head, 0)


SMEM = pl.BlockSpec(memory_space=pltpu.SMEM)
VMEM = pl.BlockSpec(memory_space=pltpu.VMEM)


def attention(jobs, ends, slabs, ext, q, arrays, own=None, state=None, other=None, paired=False):
    rows, feat = q.shape
    scale = math.log2(math.e) / math.sqrt(HW)
    spec = (jobs, own is not None, ends, slabs, len(arrays), paired, scale)
    args = [ext, q] + list(own if own is not None else state) + list(arrays)
    if other is not None:
        args.append(other)
    part = jax.ShapeDtypeStruct((rows, HW), jnp.float32)
    if ends == "state":
        outs = (part,) * 3
    elif ends == "split":
        outs = (part,) * 3 + (jax.ShapeDtypeStruct((rows, HW), jnp.bfloat16),)
    else:
        outs = jax.ShapeDtypeStruct((rows, feat), jnp.bfloat16)
    scores = rows * rows * (sum(len(s[2]) for s in slabs) + 1)
    return pl.pallas_call(
        functools.partial(attention_kernel, spec),
        out_shape=outs,
        in_specs=[SMEM] + [VMEM] * (len(args) - 1),
        out_specs=(VMEM,) * len(outs) if isinstance(outs, tuple) else VMEM,
        scratch_shapes=[pltpu.VMEM((rows, HW), jnp.float32)] * 3,
        compiler_params=pltpu.CompilerParams(vmem_limit_bytes=40 * 1024 * 1024),
        cost_estimate=pl.CostEstimate(
            flops=4 * HW * scores, bytes_accessed=4 * rows * feat * 4, transcendentals=scores
        ),
    )(*args)


def pick_kernel(ext_ref, k_ref, v_ref, h_ref, t_ref):
    for out_ref, axis in ((h_ref, 1), (t_ref, 0)):
        cols = pl.ds(pl.multiple_of((1 - ext_ref[0, axis]) * HW, HW), HW)
        out_ref[:, :HW] = k_ref[:, cols]
        out_ref[:, HW:] = v_ref[:, cols]


def pick(ext, k, v):
    rows = k.shape[0]
    part = jax.ShapeDtypeStruct((rows, 2 * HW), k.dtype)
    return pl.pallas_call(
        pick_kernel,
        in_specs=[SMEM, VMEM, VMEM],
        out_specs=(VMEM, VMEM),
        out_shape=(part, part),
        cost_estimate=pl.CostEstimate(flops=0, bytes_accessed=16 * rows * HW, transcendentals=0),
        name="pick",
    )(ext, k, v)


def shards(video_q, video_k, video_v, text_k, text_v, text_valid, extent):
    rows, feat = video_q.shape[2:]
    q, k, v = (a.reshape(rows, feat) for a in (video_q, video_k, video_v))
    hn = lax.axis_size("height")
    t_rings, h_rings = rings("tm"), rings("height")
    valid = text_valid.reshape(1, -1)

    table = 0
    for c in range(16):
        t0, h0, t1, h1 = (c >> i & 1 for i in range(4))
        crowded = (t0 and t1) or (h0 and h1)
        table |= (2 if crowded else int((t0 and h0) or (t1 and h1))) << (2 * c)
    table -= (table >> 31) << 32
    shift = jnp.sum(extent * jnp.array([[2, 4, 0], [8, 16, 0]], jnp.int32))
    branch = lax.shift_right_arithmetic(jnp.int32(table), shift) & 3

    def text_tokens(text_k, text_v):
        mine = jnp.concatenate([text_k, text_v], axis=1)
        copies = jnp.broadcast_to(mine[None], (hn,) + mine.shape)
        got = lax.all_to_all(copies, "height", 0, 0)
        return got.reshape(-1, mine.shape[1])

    def exchange(x, axis, pairs):
        up, down = pairs
        before = lax.ppermute(x, axis, up)
        after = lax.ppermute(x, axis, down)
        return before, after

    def sparse(diagonal):
        def run(q, k, v, text_k, text_v, valid, ext):
            kv_h, kv_t = pick(ext, k, v)
            h0, h1 = exchange(kv_h, "height", h_rings)
            t0, t1 = exchange(kv_t, "tm", t_rings)
            text = text_tokens(text_k, text_v)
            m, l, a, other = attention(
                2, "split", ((True, False, ((0, 0, -1, 0), (1, 0, 1, 0))),),
                ext, q, (t0, t1), own=(k, v, text, valid),
            )
            hs = ((False, True, ((0, 0, 0, -1), (1, 0, 0, 1))),)
            if not diagonal:
                return attention(1, "merge", hs, ext, q, (h0, h1), state=(m, l, a), other=other)
            d0, d1 = exchange(jnp.concatenate([h0, h1], axis=0), "tm", t_rings)
            m, l, a = attention(1, "state", hs, ext, q, (h0, h1), state=(m, l, a))
            corners = ((0, 0, -1, -1), (0, rows, -1, 1), (1, 0, 1, -1), (1, rows, 1, 1))
            ds = ((True, True, corners),)
            return attention(
                1, "merge", ds, ext, q, (d0, d1),
                state=(m, l, a), other=other,
            )

        return run

    def dense(q, k, v, text_k, text_v, valid, ext):
        kv = jnp.concatenate([k, v], axis=1)
        h0, h1 = exchange(kv, "height", h_rings)
        text = text_tokens(text_k, text_v)
        three = jnp.concatenate([h0, kv, h1], axis=0)
        t0, t1 = exchange(three, "tm", t_rings)
        slabs = (
            (False, True, ((0, 0, 0, -1), (1, 0, 0, 1))),
            (True, False, ((2, rows, -1, 0), (3, rows, 1, 0))),
            (True, True, ((2, 0, -1, -1), (2, 2 * rows, -1, 1))),
            (True, True, ((3, 0, 1, -1), (3, 2 * rows, 1, 1))),
        )
        return attention(
            2, "all", slabs, ext, q, (h0, h1, t0, t1),
            own=(k, v, text, valid), paired=True,
        )

    out = lax.switch(
        branch, [sparse(False), sparse(True), dense], q, k, v, text_k, text_v, valid, extent
    )
    return out.reshape(video_q.shape)


def solution(mesh):
    video = P("tm", "height", None, None)
    return jax.shard_map(
        shards,
        mesh=mesh,
        in_specs=(video, video, video, P("height", None), P("height", None), P(), P()),
        out_specs=video,
        check_vma=False,
    )
```
